256 devices in a mesh: py: 8 (over z_lo, core), px: 32 (over y, z_hi, x).
Axes of the slice: x: 4, y: 4, z: 8 (z_hi: 2, z_lo: 4; z = z_hi * 4 + z_lo), core: 2. Of those that a mesh axis runs over, the one named last changes fastest.
Arguments:
- measured: float32 [2, 2, 8, 32, 12544], P(None, None, 'py', 'px'), may hold values from -250 to 250
- psf_taps: bfloat16 [8, 32, 32, 32, 32], P('py', 'px'), may hold values from 0 to 0.011047363
- offsets: int32 [8, 32, 2], P('py', 'px'), may hold values from 0 to 7
- window_mask: int32 [1024, 4096], P('py', 'px'), may hold values 0 or 1
Outputs:
- object_basis: float32 [2, 2, 8, 32, 12544], P(None, None, 'py', 'px')
- image_basis: float32 [2, 2, 8, 32, 12544], P(None, None, 'py', 'px')
- factors: float32 [3, 2, 2], replicated
The draws below stay inside these ranges and needn't reach their ends.
All inputs are finite; a program needn't handle non-finite values. No bound on the sum of `window_mask` on one device may be relied on, other than what follows from the above.
Results may differ from the reference program's by a relative error of at most 0.014.
Values may be sent and summed in bfloat16 or wider, within the bound.
A program may use at most 128 MiB of HBM per device.

```python
import math
import jax
import jax.numpy as jnp
from jax import lax

PLANES = 2
PATCH = 128
KERNEL = 32
DEPTH_LEN = 64
HALF = 8
CORE = 112
HEIGHT = 896
WIDTH = 3584
N_PY = 8
N_PX = 32


def draw_measured(key, part):
    first_key = jax.random.fold_in(key, 11)
    rows_pos = jnp.arange(HEIGHT, dtype=jnp.float32)[:, None] / HEIGHT
    cols_pos = jnp.arange(WIDTH, dtype=jnp.float32)[None, :] / WIDTH
    column_scale = jnp.array([1.0, 3.0], jnp.float32)[:, None, None, None]
    spread = 10.0 ** (0.5 * (rows_pos + cols_pos))
    stacked = jax.random.truncated_normal(first_key, -4.0, 4.0, (2, PLANES, HEIGHT, WIDTH), jnp.float32)
    field = (stacked * spread * column_scale).astype(jnp.float32)
    blocks = field.reshape(2, PLANES, N_PY, CORE, N_PX, CORE)
    return blocks.transpose(0, 1, 2, 4, 3, 5).reshape(2, PLANES, N_PY, N_PX, CORE * CORE)


def plant(drawn, key, least, top_value):
    longest = drawn.shape.index(max(drawn.shape))
    spots = []
    for shift in (0, 1):
        where = [jax.random.randint(jax.random.fold_in(key, axis), (), 0, length) for axis, length in enumerate(drawn.shape)]
        where[longest] = (where[longest] + shift) % drawn.shape[longest]
        spots.append(tuple(where))
    return drawn.at[spots[0]].set(least).at[spots[1]].set(top_value)


def block_levels(key, extent, shards, least, high):
    def one(position, shards_of):
        draws = jax.random.uniform(jax.random.fold_in(jax.random.fold_in(key, 6), position), (shards_of,), jnp.float32, least / len(shards), high / len(shards))
        return jnp.repeat(jnp.exp(draws), extent[position] // shards_of).reshape((-1,) + (1,) * (len(extent) - position - 1))

    level = one(*shards[0])
    for cut in shards[1:]:
        level = level * one(*cut)
    return level


def setup_inputs(seed: int = 0) -> dict:
    key_of = jax.random.split(jax.random.key(seed), 5)
    return {
        "measured": draw_measured(jax.random.fold_in(key_of[4], 71), 0),
        "psf_taps": jnp.clip(0.011047363 * jax.random.uniform(key_of[1], (N_PY, N_PX, KERNEL, KERNEL, KERNEL), jnp.float32) ** block_levels(key_of[1], (N_PY, N_PX, KERNEL, KERNEL, KERNEL), ((0, 8), (1, 32)), -0.2, 0.2), 0.0, 0.011047363).astype(jnp.bfloat16),
        "offsets": plant(jax.random.randint(key_of[2], (N_PY, N_PX, 2), 0, 8), jax.random.fold_in(key_of[2], 1), 0, 7).astype(jnp.int32),
        "window_mask": plant((jax.random.randint(key_of[3], (N_PY * PATCH, N_PX * PATCH), 0, 8) < 7).astype(jnp.int32), jax.random.fold_in(key_of[3], 1), 0, 1),
    }


epsilon = 1e-06

def to_grid(stored):
    blocks = stored.reshape(2, PLANES, N_PY, N_PX, CORE, CORE)
    return blocks.transpose(0, 1, 2, 4, 3, 5).reshape(2, PLANES, HEIGHT, WIDTH)

def to_tiles(field):
    blocks = field.reshape(2, PLANES, N_PY, CORE, N_PX, CORE)
    return blocks.transpose(0, 1, 2, 4, 3, 5).reshape(2, PLANES, N_PY, N_PX, CORE * CORE)

def twiddle(rows, cols, length, shift):
    row_ids = jnp.arange(rows, dtype=jnp.int32)[:, None]
    col_ids = jnp.arange(cols, dtype=jnp.int32)[None, :] + jnp.asarray(shift).astype(jnp.int32)
    phase = row_ids * col_ids % length
    angle = phase.astype(jnp.float32) * jnp.float32(2.0 * math.pi / length)
    return (jnp.cos(angle).astype(jnp.bfloat16), (-jnp.sin(angle)).astype(jnp.bfloat16))

def product(form, table, values):
    return jnp.einsum(form, table.astype(jnp.float32), values.astype(jnp.float32))

def complex_axis(form, cos_table, sin_table, real_in, imag_in):
    real_out = product(form, cos_table, real_in) - product(form, sin_table, imag_in)
    imag_out = product(form, cos_table, imag_in) + product(form, sin_table, real_in)
    return (real_out.astype(jnp.bfloat16), imag_out.astype(jnp.bfloat16))

def spectrum(patch_taps, shift_rows, shift_cols):
    half_kernel = KERNEL // 2
    cos_x, sin_x = twiddle(PATCH, KERNEL, PATCH, shift_cols - half_kernel)
    real_x = product('fi,tji->tjf', cos_x, patch_taps).astype(jnp.bfloat16)
    imag_x = product('fi,tji->tjf', sin_x, patch_taps).astype(jnp.bfloat16)
    cos_y, sin_y = twiddle(PATCH, KERNEL, PATCH, shift_rows - half_kernel)
    real_y, imag_y = complex_axis('gj,tjf->tgf', cos_y, sin_y, real_x, imag_x)
    cos_z, sin_z = twiddle(DEPTH_LEN, KERNEL, DEPTH_LEN, -half_kernel)
    return complex_axis('qt,tgf->qgf', cos_z, sin_z, real_y, imag_y)

def blur(patch_cells, spec_real, spec_imag, adjoint):
    values = patch_cells.astype(jnp.bfloat16)
    cos_p, sin_p = twiddle(PATCH, PATCH, PATCH, 0)
    real_x = product('fx,bzyx->bzyf', cos_p, values).astype(jnp.bfloat16)
    imag_x = product('fx,bzyx->bzyf', sin_p, values).astype(jnp.bfloat16)
    real_y, imag_y = complex_axis('gy,bzyf->bzgf', cos_p, sin_p, real_x, imag_x)
    cos_z, sin_z = twiddle(DEPTH_LEN, PLANES, DEPTH_LEN, 0)
    depth_re, depth_im = complex_axis('qz,bzgf->bqgf', cos_z, sin_z, real_y, imag_y)
    kernel_re = spec_real.astype(jnp.float32)
    kernel_im = spec_imag.astype(jnp.float32)
    if adjoint:
        kernel_im = -kernel_im
    depth_re = depth_re.astype(jnp.float32)
    depth_im = depth_im.astype(jnp.float32)
    prod_re = (depth_re * kernel_re - depth_im * kernel_im).astype(jnp.bfloat16)
    prod_im = (depth_re * kernel_im + depth_im * kernel_re).astype(jnp.bfloat16)
    back_cos, back_sin = twiddle(PLANES, DEPTH_LEN, DEPTH_LEN, 0)
    plane_re, plane_im = complex_axis('zq,bqgf->bzgf', back_cos, -back_sin, prod_re, prod_im)
    row_re, row_im = complex_axis('yg,bzgf->bzyf', cos_p, -sin_p, plane_re, plane_im)
    spatial = product('xf,bzyf->bzyx', cos_p, row_re) + product('xf,bzyf->bzyx', sin_p, row_im)
    return spatial * jnp.float32(1.0 / (DEPTH_LEN * PATCH * PATCH))

def window(mask_block):
    return mask_block.astype(jnp.float32)

def apply_all(field, psf_taps, offsets, window_mask, adjoint):
    padded = jnp.pad(field, ((0, 0), (0, 0), (HALF, HALF), (HALF, HALF)))

    def add_patch(patch_id, summed):
        patch_row = (patch_id // N_PX).astype(jnp.int32)
        patch_col = (patch_id % N_PX).astype(jnp.int32)
        nought = jnp.zeros((), jnp.int32)
        corner = (nought, nought, patch_row * CORE, patch_col * CORE)
        patch_cells = lax.dynamic_slice(padded, corner, (2, PLANES, PATCH, PATCH))
        mask_block = lax.dynamic_slice(window_mask, (patch_row * PATCH, patch_col * PATCH), (PATCH, PATCH))
        weight = window(mask_block)
        patch_taps = psf_taps[patch_row, patch_col]
        shifts = offsets[patch_row, patch_col]
        spec_real, spec_imag = spectrum(patch_taps, shifts[0], shifts[1])
        if adjoint:
            result = blur(patch_cells, spec_real, spec_imag, True) * weight
        else:
            result = blur(patch_cells * weight, spec_real, spec_imag, False)
        previous = lax.dynamic_slice(summed, corner, (2, PLANES, PATCH, PATCH))
        return lax.dynamic_update_slice(summed, previous + result, corner)
    summed = lax.fori_loop(0, N_PY * N_PX, add_patch, jnp.zeros_like(padded))
    return summed[:, :, HALF:HALF + HEIGHT, HALF:HALF + WIDTH]

def factor(pair, count):
    g_first = jnp.sum(pair[0] * pair[0]) / count
    g_cross = jnp.sum(pair[0] * pair[1]) / count
    g_second = jnp.sum(pair[1] * pair[1]) / count
    r_first = jnp.sqrt(g_first + epsilon)
    r_cross = g_cross / r_first
    r_second = jnp.sqrt(g_second - r_cross * r_cross + epsilon)
    return (r_first, r_cross, r_second)

def solve_right(pair, triple):
    leading = pair[0] / triple[0]
    trailing = (pair[1] - triple[1] * leading) / triple[2]
    return jnp.stack([leading, trailing])

def packed(triple):
    return jnp.stack([jnp.stack([triple[0], triple[1]]), jnp.stack([jnp.zeros_like(triple[0]), triple[2]])])

def reference(measured, psf_taps, offsets, window_mask):
    count = jnp.float32(PLANES * HEIGHT * WIDTH)
    measured_grid = to_grid(measured)
    start_factor = factor(measured_grid, count)
    left_basis = solve_right(measured_grid, start_factor)
    adjoint_field = apply_all(left_basis, psf_taps, offsets, window_mask, True)
    alpha_factor = factor(adjoint_field, count)
    object_basis = solve_right(adjoint_field, alpha_factor)
    forward_field = apply_all(object_basis, psf_taps, offsets, window_mask, False)
    residue = jnp.stack([forward_field[0] - alpha_factor[0] * left_basis[0] - alpha_factor[1] * left_basis[1], forward_field[1] - alpha_factor[2] * left_basis[1]])
    beta_factor = factor(residue, count)
    image_basis = solve_right(residue, beta_factor)
    factors = jnp.stack([packed(start_factor), packed(alpha_factor), packed(beta_factor)])
    return (to_tiles(object_basis), to_tiles(image_basis), factors)
```

```python
import functools
import math

import jax
import jax.numpy as jnp
import numpy as np
from jax import lax
from jax.experimental import pallas as pl
from jax.experimental.pallas import tpu as pltpu
from jax.sharding import PartitionSpec as P

PLANES = 2
PATCH = 128
KERNEL = 32
DEPTH_LEN = 64
HALF = 8
CORE = 112


epsilon = 1e-06


def padded_2(shard, sides, width):
    for axis, dim in sides:
        size, length = (lax.axis_size(axis), shard.shape[dim])
        up = [(i, (i + 1) % size) for i in range(size - 1)]
        down = [(j, i) for i, j in up]
        last = lax.slice_in_dim(shard, length - width, length, axis=dim)
        leading = lax.slice_in_dim(shard, 0, width, axis=dim)
        before = lax.ppermute(last, axis, up)
        after = lax.ppermute(leading, axis, down)
        shard = jnp.concatenate([before, shard, after], axis=dim)
    return shard


def roots(rows, cols, length):
    phase = np.outer(np.asarray(rows), np.asarray(cols)) % length
    angle = phase * (2.0 * math.pi / length)
    return (np.cos(angle).astype(jnp.bfloat16), (-np.sin(angle)).astype(jnp.bfloat16))


def depth_mix():
    shifted = np.arange(KERNEL) - KERNEL // 2
    depths = np.arange(DEPTH_LEN)
    cos_t, sin_t = (part.astype(np.float64) for part in roots(depths, shifted, DEPTH_LEN))
    cos_z, sin_z = (
        part.astype(np.float64) for part in roots(depths, np.arange(PLANES), DEPTH_LEN)
    )
    taps = cos_t + 1j * sin_t
    ahead = cos_z + 1j * sin_z
    mix = np.einsum("qo,qz,qt->ozt", np.conj(ahead), ahead, taps)
    return np.stack([mix.real, mix.imag]).astype(np.float32)


def product(form, table, values):
    return jnp.einsum(form, table, values, preferred_element_type=jnp.float32)


def complex_axis(form, cos_table, sin_table, real_in, imag_in):
    real_out = product(form, cos_table, real_in) - product(form, sin_table, imag_in)
    imag_out = product(form, cos_table, imag_in) + product(form, sin_table, real_in)
    return (real_out, imag_out)


def narrow(pair):
    return (pair[0].astype(jnp.bfloat16), pair[1].astype(jnp.bfloat16))


def shifted_roots(shift):
    half_kernel = KERNEL // 2
    cos_all, sin_all = roots(np.arange(KERNEL + 8) - half_kernel, np.arange(PATCH), PATCH)
    return (
        lax.dynamic_slice_in_dim(jnp.asarray(cos_all), shift, KERNEL, axis=0),
        lax.dynamic_slice_in_dim(jnp.asarray(sin_all), shift, KERNEL, axis=0),
    )


def spectrum(patch_taps, shift_rows, shift_cols):
    mixed = jnp.einsum(
        "cozt,tji->cozji",
        depth_mix(),
        patch_taps.astype(jnp.float32),
        precision=lax.Precision.HIGHEST,
    )
    mixed_re, mixed_im = narrow((mixed[0], mixed[1]))
    cos_x, sin_x = shifted_roots(shift_cols)
    real_x, imag_x = narrow(complex_axis("if,ozji->ozjf", cos_x, sin_x, mixed_re, mixed_im))
    cos_y, sin_y = shifted_roots(shift_rows)
    return complex_axis("jg,ozjf->ozgf", cos_y, sin_y, real_x, imag_x)


def blur(patch_cells, spec_real, spec_imag, adjoint):
    values = patch_cells.astype(jnp.bfloat16)
    cos_p, sin_p = roots(np.arange(PATCH), np.arange(PATCH), PATCH)
    real_x = product("fx,bzyx->bzyf", cos_p, values).astype(jnp.bfloat16)
    imag_x = product("fx,bzyx->bzyf", sin_p, values).astype(jnp.bfloat16)
    real_y, imag_y = complex_axis("gy,bzyf->bzgf", cos_p, sin_p, real_x, imag_x)
    planes_re, planes_im = [], []
    for out in range(PLANES):
        total_re, total_im = 0.0, 0.0
        for z in range(PLANES):
            if adjoint:
                kernel_re, kernel_im = spec_real[z, out], -spec_imag[z, out]
            else:
                kernel_re, kernel_im = spec_real[out, z], spec_imag[out, z]
            total_re = total_re + real_y[:, z] * kernel_re - imag_y[:, z] * kernel_im
            total_im = total_im + real_y[:, z] * kernel_im + imag_y[:, z] * kernel_re
        planes_re.append(total_re)
        planes_im.append(total_im)
    plane_re, plane_im = narrow((jnp.stack(planes_re, axis=1), jnp.stack(planes_im, axis=1)))
    row_re, row_im = narrow(complex_axis("yg,bzgf->bzyf", cos_p, -sin_p, plane_re, plane_im))
    spatial = product("xf,bzyf->bzyx", cos_p, row_re) + product("xf,bzyf->bzyx", sin_p, row_im)
    return spatial * jnp.float32(1.0 / (DEPTH_LEN * PATCH * PATCH))


def gather_kernel(rows, cols, x_ref, out_ref, first, mid, second, send_r, recv_r, send_c, recv_c):
    my_row, my_col = lax.axis_index("py"), lax.axis_index("px")
    barrier = pltpu.get_barrier_semaphore()

    def greet_row(step, carry):
        pl.semaphore_signal(
            barrier,
            inc=1,
            device_id=((my_row + step) % rows, my_col),
            device_id_type=pl.DeviceIdType.MESH,
        )
        return carry

    def greet_col(step, carry):
        pl.semaphore_signal(
            barrier,
            inc=1,
            device_id=(my_row, (my_col + step) % cols),
            device_id_type=pl.DeviceIdType.MESH,
        )
        return carry

    lax.fori_loop(1, rows, greet_row, 0)
    lax.fori_loop(1, cols, greet_col, 0)
    pl.semaphore_wait(barrier, rows + cols - 2)

    def row_copy(step):
        return pltpu.make_async_remote_copy(
            src_ref=x_ref,
            dst_ref=first.at[step],
            send_sem=send_r.at[step],
            recv_sem=recv_r.at[step],
            device_id=((my_row + step) % rows, my_col),
            device_id_type=pl.DeviceIdType.MESH,
        )

    def col_copy(step):
        return pltpu.make_async_remote_copy(
            src_ref=mid,
            dst_ref=second.at[step],
            send_sem=send_c.at[step],
            recv_sem=recv_c.at[step],
            device_id=(my_row, (my_col + step) % cols),
            device_id_type=pl.DeviceIdType.MESH,
        )

    def start(copy):
        def run(step, carry):
            copy(step).start()
            return carry

        return run

    def finish(copy):
        def run(step, carry):
            copy(step).wait()
            return carry

        return run

    def ordered(own, slots, mine, size):
        def run(index, total):
            slot = (mine - index + size) % size
            return total + slots[slot]

        return lax.fori_loop(0, size, run, jnp.zeros_like(own))

    lax.fori_loop(1, rows, start(row_copy), 0)
    first[0] = x_ref[...]
    lax.fori_loop(1, rows, finish(row_copy), 0)
    summed = ordered(x_ref[...], first, my_row, rows)
    mid[...] = summed
    second[0] = summed
    lax.fori_loop(1, cols, start(col_copy), 0)
    lax.fori_loop(1, cols, finish(col_copy), 0)
    out_ref[...] = ordered(summed, second, my_col, cols)


def total_sum(terms):
    rows, cols = lax.axis_size("py"), lax.axis_size("px")
    lane = lax.broadcasted_iota(jnp.int32, (8, PATCH), 1)
    tile = jnp.where(lane == 0, terms[0], jnp.where(lane == 1, terms[1], terms[2]))
    tile = pl.pallas_call(
        functools.partial(gather_kernel, rows, cols),
        out_shape=jax.ShapeDtypeStruct((8, PATCH), jnp.float32),
        in_specs=[pl.BlockSpec(memory_space=pltpu.VMEM)],
        out_specs=pl.BlockSpec(memory_space=pltpu.VMEM),
        scratch_shapes=[
            pltpu.VMEM((rows, 8, PATCH), jnp.float32),
            pltpu.VMEM((8, PATCH), jnp.float32),
            pltpu.VMEM((cols, 8, PATCH), jnp.float32),
            pltpu.SemaphoreType.DMA((rows,)),
            pltpu.SemaphoreType.DMA((rows,)),
            pltpu.SemaphoreType.DMA((cols,)),
            pltpu.SemaphoreType.DMA((cols,)),
        ],
        compiler_params=pltpu.CompilerParams(collective_id=0, has_side_effects=True),
        name="gather_sum",
    )(tile)
    return (tile[0, 0], tile[0, 1], tile[0, 2])


def window(mask_block):
    return mask_block.astype(jnp.float32)


def fold_owned(padded, dim):
    lower = lax.slice_in_dim(padded, 0, HALF, axis=dim) + lax.slice_in_dim(
        padded, 2 * HALF, 3 * HALF, axis=dim
    )
    middle = lax.slice_in_dim(padded, 3 * HALF, PATCH - HALF, axis=dim)
    upper = lax.slice_in_dim(padded, PATCH - HALF, PATCH, axis=dim) + lax.slice_in_dim(
        padded, PATCH + HALF, PATCH + 2 * HALF, axis=dim
    )
    return jnp.concatenate([lower, middle, upper], axis=dim)


def gram_terms(pair):
    return (jnp.sum(pair[0] * pair[0]), jnp.sum(pair[0] * pair[1]), jnp.sum(pair[1] * pair[1]))


def factor(terms, count):
    r_first = jnp.sqrt(terms[0] / count + epsilon)
    r_cross = terms[1] / count / r_first
    r_second = jnp.sqrt(terms[2] / count - r_cross * r_cross + epsilon)
    return (r_first, r_cross, r_second)


def solve_right(pair, triple):
    leading = pair[0] / triple[0]
    trailing = (pair[1] - triple[1] * leading) / triple[2]
    return jnp.stack([leading, trailing])


def packed(triple):
    return jnp.stack(
        [jnp.stack([triple[0], triple[1]]), jnp.stack([jnp.zeros_like(triple[0]), triple[2]])]
    )


def flatten_cells(block):
    return block.reshape(2, PLANES, 1, 1, CORE * CORE)


def body(measured, psf_taps, offsets, window_mask):
    count_rows = lax.axis_size("py")
    count_cols = lax.axis_size("px")
    count = jnp.float32(PLANES * CORE * CORE * count_rows * count_cols)
    spec_real, spec_imag = spectrum(psf_taps[0, 0], offsets[0, 0, 0], offsets[0, 0, 1])
    weight = window(window_mask)
    first_sq, first_cross, first_tail = gram_terms(measured)
    start_terms = total_sum((first_sq, first_cross, first_tail))
    start_factor = factor(start_terms, count)
    left_flat = solve_right(measured, start_factor)
    left_basis = left_flat.reshape(2, PLANES, CORE, CORE)
    left_narrow = left_basis.astype(jnp.bfloat16)
    left_patch = padded_2(left_narrow, (("py", 2), ("px", 3)), HALF)
    adjoint_patch = blur(left_patch, spec_real, spec_imag, True) * weight
    folded = padded_2(adjoint_patch, (("py", 2), ("px", 3)), HALF)
    adjoint_core = fold_owned(fold_owned(folded, 2), 3)
    second_sq, second_cross, second_tail = gram_terms(adjoint_core)
    alpha_terms = total_sum((second_sq, second_cross, second_tail))
    alpha_factor = factor(alpha_terms, count)
    object_basis = solve_right(adjoint_core, alpha_factor)
    object_patch = padded_2(object_basis, (("py", 2), ("px", 3)), HALF)
    forward_patch = blur(object_patch * weight, spec_real, spec_imag, False)
    forward_padded = padded_2(forward_patch, (("py", 2), ("px", 3)), HALF)
    forward_core = fold_owned(fold_owned(forward_padded, 2), 3)
    residue = jnp.stack(
        [
            forward_core[0] - alpha_factor[0] * left_basis[0] - alpha_factor[1] * left_basis[1],
            forward_core[1] - alpha_factor[2] * left_basis[1],
        ]
    )
    third_sq, third_cross, third_tail = gram_terms(residue)
    beta_terms = total_sum((third_sq, third_cross, third_tail))
    beta_factor = factor(beta_terms, count)
    image_basis = solve_right(residue, beta_factor)
    factors = jnp.stack([packed(start_factor), packed(alpha_factor), packed(beta_factor)])
    return (flatten_cells(object_basis), flatten_cells(image_basis), factors)


def solution(mesh):
    placed = (
        P(None, None, "py", "px", None),
        P("py", "px", None, None, None),
        P("py", "px", None),
        P("py", "px"),
    )
    return jax.shard_map(
        body,
        mesh=mesh,
        in_specs=placed,
        out_specs=(P(None, None, "py", "px", None), P(None, None, "py", "px", None), P()),
        check_vma=False,
    )
```
